128 devices in a mesh: clip: 8 (over z, core), seq: 16 (over x, y).
Axes of the slice: x: 4, y: 4, z: 4, core: 2. Of those that a mesh axis runs over, the one named last changes fastest.
Arguments:
- query_in: bfloat16 [16384, 4096], P(('clip', 'seq')), parts along dimension 0, may hold values from -12 to 12
- key_in: bfloat16 [16384, 4096], P(('clip', 'seq')), parts along dimension 0, may hold values from -12 to 12
- value_in: bfloat16 [16384, 4096], P(('clip', 'seq')), parts along dimension 0, may hold values from -6 to 6
- grad_out: bfloat16 [16384, 4096], P(('clip', 'seq')), parts along dimension 0, may hold values from -6 to 6
- positions: int32 [3, 16384], P(None, 'clip'), parts along dimension 1, may hold values from 0 to 15, as said below
- block_flags: int32 [128, 16], P('clip'), parts along dimension 0, may hold values from 0 to 1, as said below
- band_ids: int32 [128, 16], P('clip'), parts along dimension 0, may hold values from 0 to 3, as said below
Outputs:
- attn_out: bfloat16 [16384, 4096], P(('clip', 'seq')), parts along dimension 0
- grad_query: bfloat16 [16384, 4096], P(('clip', 'seq')), parts along dimension 0
- grad_key: bfloat16 [16384, 4096], P(('clip', 'seq')), parts along dimension 0
- grad_value: bfloat16 [16384, 4096], P(('clip', 'seq')), parts along dimension 0
The draws below stay inside these ranges and needn't reach their ends.
There are 8 independent parts, one for each index of `clip`. The reference program is written for one: setup_inputs(seed, part) draws one part's arguments, and reference() takes and returns one part's arrays. A program takes and returns all parts, laid end to end along the dimension named above; each array names one. Nothing has to cross between parts.
Inputs may be any that keep to these rules, and one draw needn't show every extreme that they name: positions[0] is the latent frame of a token: tokens come in frames of 256, frame numbers rise strictly from frame to frame and may skip, and the last frame's number is 15; positions[1] and positions[2] are row and column in a square crop, row-major. `block_flags`: diagonal block pairs are always 1. `band_ids`: diagonal block pairs are 0.
All inputs are finite; a program needn't handle non-finite values.
Results may differ from the reference program's by a relative error of at most 0.015.
Values may be sent and summed in bfloat16 or wider, within the bound.
A program may use at most 128 MiB of HBM per device.

```python
import math
import jax
import jax.numpy as jnp
from jax import lax

H = 32
DH = 128
BLK = 128
FRAME_TOK = 256
TOKENS = 2048


def queries_and_keys(key):
    shape_all = (TOKENS, H * DH)
    query_all = jax.random.truncated_normal(jax.random.fold_in(key, 1), -6.0, 6.0, shape_all, jnp.float32)
    key_all = jax.random.truncated_normal(jax.random.fold_in(key, 2), -6.0, 6.0, shape_all, jnp.float32)
    return (query_all, key_all)


def draw_query_in(key, part):
    return queries_and_keys(key)[0].astype(jnp.bfloat16)


def draw_key_in(key, part):
    return queries_and_keys(key)[1].astype(jnp.bfloat16)


def draw_positions(key, part):
    frames_all = TOKENS // FRAME_TOK
    order = jax.random.permutation(jax.random.fold_in(key, 21), 2 * frames_all - 1)[:frames_all - 1]
    earlier_frames = jnp.sort(order).astype(jnp.int32)
    last_frame = jnp.full((1,), 2 * frames_all - 1, jnp.int32)
    chosen_frames = jnp.concatenate([earlier_frames, last_frame], 0)
    row_ids = jnp.arange(TOKENS, dtype=jnp.int32)
    side_len = int(math.isqrt(FRAME_TOK))
    frame_num = chosen_frames[row_ids // FRAME_TOK]
    row_num = row_ids % FRAME_TOK // side_len
    column_num = row_ids % side_len
    return jnp.stack([frame_num, row_num, column_num], 0).astype(jnp.int32)


def mask_pair(key):
    blocks_all = TOKENS // BLK
    per_frame = FRAME_TOK // BLK
    block_ids = jnp.arange(blocks_all, dtype=jnp.int32)
    frame_gap = jnp.abs(block_ids[:, None] // per_frame - block_ids[None, :] // per_frame)
    level = (frame_gap >= 1).astype(jnp.int32) + (frame_gap >= 2).astype(jnp.int32) + (frame_gap >= 4).astype(jnp.int32)
    extra = jax.random.randint(jax.random.fold_in(key, 31), (blocks_all, blocks_all), 0, 2)
    diagonal = block_ids[:, None] == block_ids[None, :]
    band_all = jnp.where(diagonal, 0, jnp.minimum(level + extra, 3)).astype(jnp.int32)
    rolled = jax.random.randint(jax.random.fold_in(key, 32), (blocks_all, blocks_all), 0, 8)
    flag_all = jnp.where(diagonal, 1, (rolled < jnp.right_shift(jnp.int32(8), band_all)).astype(jnp.int32)).astype(jnp.int32)
    return (flag_all, band_all)


def draw_block_flags(key, part):
    return mask_pair(key)[0]


def draw_band_ids(key, part):
    return mask_pair(key)[1]


def level_of(stream_key, extent, shards, smallest, top_value):
    loudness, own = 1.0, jax.random.fold_in(stream_key, 6)
    for dim, parts in shards:
        heights = jnp.exp(jax.random.uniform(jax.random.fold_in(own, dim), (parts,), jnp.float32, smallest / len(shards), top_value / len(shards)))
        loudness = loudness * jnp.repeat(heights, extent[dim] // parts).reshape([-1 if axis == dim else 1 for axis in range(len(extent))])
    return loudness


def bell_draw(key, shape, spread, limit, pieces=(), kind=jnp.bfloat16):
    result = spread * jax.random.normal(key, shape, jnp.float32)
    if pieces:
        result = result * level_of(key, shape, pieces, -0.22, 0.18)
    return jnp.clip(result, -limit, limit).astype(kind)


def setup_inputs(seed: int = 0, part: int = 0) -> dict:
    seeds = jax.random.split(jax.random.key(seed), 8)
    part_splits = jax.random.split(jax.random.fold_in(seeds[7], part), 8)
    query_in = draw_query_in(jax.random.fold_in(jax.random.fold_in(seeds[7], part), 71), part)
    key_in = draw_key_in(jax.random.fold_in(jax.random.fold_in(seeds[7], part), 71), part)
    value_in = bell_draw(part_splits[2], (TOKENS, H * DH), 1.0, 6.0, ((0, 16),))
    grad_out = bell_draw(part_splits[3], (TOKENS, H * DH), 1.0, 6.0, ((0, 16),))
    positions = draw_positions(jax.random.fold_in(jax.random.fold_in(seeds[7], part), 71), part)
    block_flags = draw_block_flags(jax.random.fold_in(jax.random.fold_in(seeds[7], part), 71), part)
    band_ids = draw_band_ids(jax.random.fold_in(jax.random.fold_in(seeds[7], part), 71), part)
    return dict(query_in=query_in, key_in=key_in, value_in=value_in, grad_out=grad_out, positions=positions, block_flags=block_flags, band_ids=band_ids)


ntk_factor = 2.0

def rope_tables(positions):
    third_part = 2 * (DH // 6)
    part_dims = (DH - 2 * third_part, third_part, third_part)
    angle_parts = []
    for axis_num, piece_dim in enumerate(part_dims):
        base_freq = 10000.0 * ntk_factor ** (piece_dim / (piece_dim - 2.0))
        pair_index = jnp.arange(piece_dim // 2, dtype=jnp.float32)
        inverse = jnp.exp(pair_index * (-2.0 * math.log(base_freq) / piece_dim))
        angle_parts.append(positions[axis_num].astype(jnp.float32)[:, None] * inverse[None, :])
    angle_all = jnp.concatenate(angle_parts, 1)
    return (jnp.cos(angle_all), jnp.sin(angle_all))

def rotate(values, cosine_table, sine_table):
    shape_all = values.shape
    paired = values.reshape(shape_all[:-1] + (shape_all[-1] // 2, 2))
    even_part = paired[..., 0]
    odd_part = paired[..., 1]
    cos_wide = cosine_table[:, None, :]
    sin_wide = sine_table[:, None, :]
    turned = jnp.stack([even_part * cos_wide - odd_part * sin_wide, odd_part * cos_wide + even_part * sin_wide], -1)
    return turned.reshape(shape_all)

def block_mask(block_flags, band_ids, first_row, row_count):
    blocks_all = block_flags.shape[1]
    rows_blocks = row_count // BLK
    start_block = first_row // BLK
    flag_rows = lax.dynamic_slice_in_dim(block_flags, start_block, rows_blocks, 0)
    band_rows = lax.dynamic_slice_in_dim(band_ids, start_block, rows_blocks, 0)
    reach_width = jnp.right_shift(jnp.int32(BLK), band_rows)
    offsets = jnp.arange(BLK, dtype=jnp.int32)
    apart_rows = jnp.abs(offsets[:, None] - offsets[None, :])
    keep_mask = (flag_rows[:, None, :, None] == 1) & (apart_rows[None, :, None, :] < reach_width[:, None, :, None])
    return keep_mask.reshape(row_count, blocks_all * BLK)

def reference(query_in, key_in, value_in, grad_out, positions, block_flags, band_ids):
    cosine_table, sine_table = rope_tables(positions)
    allowed = block_mask(block_flags, band_ids, 0, TOKENS)
    score_scale = 1.0 / math.sqrt(DH)

    def split_heads(operand):
        return operand.reshape(TOKENS, H, DH).transpose(1, 0, 2)

    def one_head(operands):
        head_query, head_key, head_value, head_grad = operands
        query_rot = rotate(head_query.astype(jnp.float32)[:, None, :], cosine_table, sine_table)[:, 0, :].astype(jnp.bfloat16)
        key_rot = rotate(head_key.astype(jnp.float32)[:, None, :], cosine_table, sine_table)[:, 0, :].astype(jnp.bfloat16)
        scores = jnp.dot(query_rot, key_rot.T, preferred_element_type=jnp.float32) * score_scale
        scores = jnp.where(allowed, scores, -jnp.inf)
        largest = lax.optimization_barrier(jnp.max(scores, axis=1, keepdims=True))
        weights = jnp.exp(scores - largest)
        probs = weights / lax.optimization_barrier(jnp.sum(weights, axis=1, keepdims=True))
        probs_low = probs.astype(jnp.bfloat16)
        attn_head = jnp.dot(probs_low, head_value, preferred_element_type=jnp.float32).astype(jnp.bfloat16)
        delta_sum = lax.optimization_barrier(jnp.sum(head_grad.astype(jnp.float32) * attn_head.astype(jnp.float32), axis=1))
        grad_probs = jnp.dot(head_grad, head_value.T, preferred_element_type=jnp.float32)
        grad_scores = (probs * (grad_probs - delta_sum[:, None]) * score_scale).astype(jnp.bfloat16)
        grad_value_head = jnp.dot(probs_low.T, head_grad, preferred_element_type=jnp.float32).astype(jnp.bfloat16)
        grad_query_rot = jnp.dot(grad_scores, key_rot, preferred_element_type=jnp.float32)
        grad_key_rot = jnp.dot(grad_scores.T, query_rot, preferred_element_type=jnp.float32)
        grad_query_head = rotate(grad_query_rot[:, None, :], cosine_table, -sine_table)[:, 0, :].astype(jnp.bfloat16)
        grad_key_head = rotate(grad_key_rot[:, None, :], cosine_table, -sine_table)[:, 0, :].astype(jnp.bfloat16)
        return (attn_head, grad_query_head, grad_key_head, grad_value_head)
    results = lax.map(one_head, (split_heads(query_in), split_heads(key_in), split_heads(value_in), split_heads(grad_out)))

    def join_heads(operand):
        return operand.transpose(1, 0, 2).reshape(TOKENS, H * DH)
    return (join_heads(results[0]), join_heads(results[1]), join_heads(results[2]), join_heads(results[3]))
```

```python
import functools
import math

import jax
import jax.numpy as jnp
import numpy as np
from jax import lax
from jax.experimental import pallas as pl
from jax.experimental.pallas import tpu as pltpu
from jax.sharding import PartitionSpec as P

H = 32
DH = 128
BLK = 128
NPOS = 16
NTK = 2.0
SIDE = 4
PEERS = 16
HEADS = 2
T = 2048
TQ = 256
CK = 512
NEG = -1e30
SCALE = 1.0 / math.sqrt(DH)
SCALE2 = SCALE * math.log2(math.e)
F32 = jnp.float32
BF16 = jnp.bfloat16
MESH_ID = pl.DeviceIdType.MESH

STEPS = (
    ((2, 1), (0, 3)),
    ((2, 3), (0, 1)),
    ((1, 2), (3, 0)),
    ((3, 2), (1, 0)),
    ((2, 2),),
    ((2, 0), (0, 2)),
    ((1, 1), (3, 3)),
    ((1, 3), (3, 1)),
)
ORDER = tuple(d for step in STEPS for d in step)


def trig_tables():
    third = 2 * (DH // 6)
    dims = (DH - 2 * third, third, third)
    cos_t = np.zeros((3 * NPOS, DH), np.float32)
    sin_t = np.zeros((3 * NPOS, DH), np.float32)
    lane = 0
    for axis, dim in enumerate(dims):
        base = 10000.0 * NTK ** (dim / (dim - 2.0))
        pair = np.arange(dim // 2, dtype=np.float32)
        inverse = np.exp(pair * np.float32(-2.0 * math.log(base) / dim)).astype(np.float32)
        angle = np.arange(NPOS, dtype=np.float32)[:, None] * inverse[None, :]
        c = np.cos(angle.astype(np.float64)).astype(np.float32)
        s = np.sin(angle.astype(np.float64)).astype(np.float32)
        rows = slice(axis * NPOS, (axis + 1) * NPOS)
        cos_t[rows, lane : lane + dim] = np.repeat(c, 2, axis=1)
        sin_t[rows, lane : lane + dim : 2] = -s
        sin_t[rows, lane + 1 : lane + dim : 2] = s
        lane += dim

    def parts(table):
        out, rest = [], table
        for _ in range(3):
            piece = rest.astype(jnp.bfloat16)
            out.append(piece)
            rest = rest - piece.astype(np.float32)
        return out

    return np.stack(parts(cos_t) + parts(sin_t), 0)


def dot(a, b, ca, cb):
    return lax.dot_general(a, b, (((ca,), (cb,)), ((), ())), preferred_element_type=F32)


def swap_pairs(x):
    even = lax.broadcasted_iota(jnp.int32, x.shape, 1) % 2 == 0
    return jnp.where(even, pltpu.roll(x, DH - 1, 1), pltpu.roll(x, 1, 1))


def kernel(
    q_in, k_in, v_in, g_in, pos_ref, flag_ref, band_ref, trig_ref,
    o_out, dq_out, dk_out, dv_out,
    land, res, cos_sc, sin_sc, bias, wexp, s_sc, w_sc, dk_acc, dv_acc,
    in_send, in_recv, out_send, out_recv, own_in, own_out,
):
    clip = lax.axis_index("clip")
    me = lax.axis_index("seq")
    mx, my = me // SIDE, me % SIDE
    sign = 1 - 2 * (clip % 2)
    ins = (q_in, k_in, v_in, g_in)
    outs = (o_out, dq_out, dk_out, dv_out)

    def peer(d):
        px = (mx + sign * d[0] + SIDE) % SIDE
        py = (my + sign * d[1] + SIDE) % SIDE
        return px * SIDE + py

    peers = [peer(d) for d in ORDER]
    barrier = pltpu.get_barrier_semaphore()
    for p in peers:
        pl.semaphore_signal(barrier, inc=1, device_id=(clip, p), device_id_type=MESH_ID)
    pl.semaphore_wait(barrier, PEERS - 1)

    def lanes(owner, h):
        return pl.ds(pl.multiple_of((owner * HEADS + h) * DH, DH), DH)

    def rows(owner):
        return pl.ds(pl.multiple_of(owner * BLK, BLK), BLK)

    def in_copy(h, a, i):
        return pltpu.make_async_remote_copy(
            src_ref=ins[a].at[:, lanes(peers[i], h)],
            dst_ref=land.at[h, a, rows(me), :],
            send_sem=in_send.at[h, a, i],
            recv_sem=in_recv.at[h, a, i],
            device_id=(clip, peers[i]),
            device_id_type=MESH_ID,
        )

    def out_copy(h, a, i):
        return pltpu.make_async_remote_copy(
            src_ref=res.at[h, a, rows(peers[i]), :],
            dst_ref=outs[a].at[:, lanes(me, h)],
            send_sem=out_send.at[h, a, i],
            recv_sem=out_recv.at[h, a, i],
            device_id=(clip, peers[i]),
            device_id_type=MESH_ID,
        )

    def own_in_copy(h, a):
        return pltpu.make_async_copy(
            ins[a].at[:, lanes(me, h)], land.at[h, a, rows(me), :], own_in.at[h, a]
        )

    def own_out_copy(h, a):
        return pltpu.make_async_copy(
            res.at[h, a, rows(me), :], outs[a].at[:, lanes(me, h)], own_out.at[h, a]
        )

    count = PEERS - 1
    for h in range(HEADS):
        for group in ((0, 1), (2, 3)):
            for i in range(count):
                for a in group:
                    in_copy(h, a, i).start()
        for a in range(4):
            own_in_copy(h, a).start()

    value = lax.broadcasted_iota(jnp.int32, (3 * NPOS, TQ), 0)

    def table_rows(t, _):
        at = pl.ds(pl.multiple_of(t * TQ, TQ), TQ)
        p = pos_ref[:, at]
        want = jnp.where(
            value < NPOS, p[0:1, :], jnp.where(value < 2 * NPOS, p[1:2, :] + NPOS, p[2:3, :] + 2 * NPOS)
        )
        hot = jnp.where(value == want, 1.0, 0.0).astype(BF16)
        cos_sc[at, :] = sum(dot(hot, trig_ref[j], 0, 0) for j in range(3))
        sin_sc[at, :] = sum(dot(hot, trig_ref[3 + j], 0, 0) for j in range(3))
        return 0

    lax.fori_loop(0, T // TQ, table_rows, 0)

    blocks = T // BLK
    band = band_ref[...]
    width = jnp.where(band == 0, 128.0, jnp.where(band == 1, 64.0, jnp.where(band == 2, 32.0, 16.0)))
    width = jnp.where(flag_ref[...] == 1, width, 0.0).astype(BF16)
    spread = lax.broadcasted_iota(jnp.int32, (blocks, T), 0) == (
        lax.broadcasted_iota(jnp.int32, (blocks, T), 1) // BLK
    )
    wexp[...] = dot(width, jnp.where(spread, 1.0, 0.0).astype(BF16), 1, 0)
    apart = jnp.abs(
        lax.broadcasted_iota(jnp.int32, (BLK, BLK), 0) - lax.broadcasted_iota(jnp.int32, (BLK, BLK), 1)
    ).astype(F32)

    def bias_rows(t, _):
        reach = wexp[pl.ds(t, 1), :]
        for j in range(blocks):
            bias[rows(t), j * BLK : (j + 1) * BLK] = jnp.where(
                apart < reach[:, j * BLK : (j + 1) * BLK], 0.0, NEG
            )
        return 0

    lax.fori_loop(0, blocks, bias_rows, 0)

    def wait_in(h, a):
        for i in range(count):
            in_copy(h, a, i).wait_recv()
        own_in_copy(h, a).wait()

    def compute(h):
        q_ref, k_ref, v_ref, g_ref = (land.at[h, a] for a in range(4))
        wait_in(h, 0)
        wait_in(h, 1)

        def turn(t, _):
            at = pl.ds(pl.multiple_of(t * TQ, TQ), TQ)
            for ref in (q_ref, k_ref):
                x = ref[at, :].astype(F32)
                ref[at, :] = (x * cos_sc[at, :] + swap_pairs(x) * sin_sc[at, :]).astype(BF16)
            return 0

        lax.fori_loop(0, T // TQ, turn, 0)
        wait_in(h, 2)
        wait_in(h, 3)
        dk_acc[...] = jnp.zeros_like(dk_acc)
        dv_acc[...] = jnp.zeros_like(dv_acc)

        def tile(t, _):
            at = pl.ds(pl.multiple_of(t * TQ, TQ), TQ)
            q = q_ref[at, :]
            g = g_ref[at, :]
            high = jnp.full((TQ, 128), -jnp.inf, F32)
            for c in range(T // CK):
                cs = pl.ds(c * CK, CK)
                s = dot(q, k_ref[cs, :], 1, 1) + bias[at, cs]
                s_sc[:, cs] = s
                for j in range(CK // 128):
                    high = jnp.maximum(high, s[:, j * 128 : (j + 1) * 128])
            m = jnp.max(high, axis=1, keepdims=True)
            total = jnp.zeros((TQ, 128), F32)
            o = jnp.zeros((TQ, DH), F32)
            for c in range(T // CK):
                cs = pl.ds(c * CK, CK)
                w = jnp.exp2((s_sc[:, cs] - m) * SCALE2)
                for j in range(CK // 128):
                    total = total + w[:, j * 128 : (j + 1) * 128]
                wb = w.astype(BF16)
                w_sc[:, cs] = wb
                o = o + dot(wb, v_ref[cs, :], 1, 0)
            inv = 1.0 / jnp.sum(total, axis=1, keepdims=True)
            gf = g.astype(F32)
            ob = (o * inv).astype(BF16)
            res[h, 0, at, :] = ob
            delta = jnp.sum(gf * ob.astype(F32), axis=1, keepdims=True) * inv
            gn = (gf * inv).astype(BF16)
            gt, qt = gn.T, q.T
            dq = jnp.zeros((TQ, DH), F32)
            for c in range(T // CK):
                cs = pl.ds(c * CK, CK)
                dp = dot(gn, v_ref[cs, :], 1, 1)
                wb = w_sc[:, cs]
                ds = (wb.astype(F32) * (dp - delta)).astype(BF16)
                dq = dq + dot(ds, k_ref[cs, :], 1, 0)
                dv_acc[:, cs] += dot(gt, wb, 1, 0)
                dk_acc[:, cs] += dot(qt, ds, 1, 0)
            dq = dq * SCALE
            dq = dq * cos_sc[at, :] - swap_pairs(dq) * sin_sc[at, :]
            res[h, 1, at, :] = dq.astype(BF16)
            return 0

        lax.fori_loop(0, T // TQ, tile, 0)
        for c in range(T // TQ):
            cs = pl.ds(c * TQ, TQ)
            dk = dk_acc[:, cs].T * SCALE
            dk = dk * cos_sc[cs, :] - swap_pairs(dk) * sin_sc[cs, :]
            res[h, 2, cs, :] = dk.astype(BF16)
            res[h, 3, cs, :] = dv_acc[:, cs].T.astype(BF16)

    for h in range(HEADS):
        compute(h)
        for i in range(count):
            for a in range(4):
                out_copy(h, a, i).start()
        for a in range(4):
            own_out_copy(h, a).start()

    for h in range(HEADS):
        for a in range(4):
            own_out_copy(h, a).wait()
            for i in range(count):
                in_copy(h, a, i).wait_send()
                out_copy(h, a, i).wait()


def body(query_in, key_in, value_in, grad_out, positions, block_flags, band_ids):
    shape = query_in.shape
    any_spec = pl.BlockSpec(memory_space=pl.ANY)
    vmem = pl.BlockSpec(memory_space=pltpu.VMEM)
    sems = pltpu.SemaphoreType.DMA((HEADS, 4, PEERS - 1))
    outs = pl.pallas_call(
        kernel,
        name="attention_exchange",
        out_shape=[jax.ShapeDtypeStruct(shape, BF16)] * 4,
        in_specs=[any_spec] * 4 + [vmem] * 4,
        out_specs=[any_spec] * 4,
        scratch_shapes=[
            pltpu.VMEM((HEADS, 4, T, DH), BF16),
            pltpu.VMEM((HEADS, 4, T, DH), BF16),
            pltpu.VMEM((T, DH), F32),
            pltpu.VMEM((T, DH), F32),
            pltpu.VMEM((T, T), F32),
            pltpu.VMEM((T // BLK, T), F32),
            pltpu.VMEM((TQ, T), F32),
            pltpu.VMEM((TQ, T), BF16),
            pltpu.VMEM((DH, T), F32),
            pltpu.VMEM((DH, T), F32),
            sems, sems, sems, sems,
            pltpu.SemaphoreType.DMA((HEADS, 4)),
            pltpu.SemaphoreType.DMA((HEADS, 4)),
        ],
        compiler_params=pltpu.CompilerParams(
            collective_id=0, has_side_effects=True, vmem_limit_bytes=60000 * 1024
        ),
    )(query_in, key_in, value_in, grad_out, positions, block_flags, band_ids, jnp.asarray(trig_tables()))
    return tuple(outs)


def solution(mesh):
    spec = P(("clip", "seq"), None)
    return jax.shard_map(
        body,
        mesh=mesh,
        in_specs=(spec, spec, spec, spec, P(None, "clip"), P("clip", None), P("clip", None)),
        out_specs=(spec, spec, spec, spec),
        check_vma=False,
    )
```

```python
import functools
import math

import jax
import jax.numpy as jnp
import numpy as np
from jax import lax
from jax.experimental import pallas as pl
from jax.experimental.pallas import tpu as pltpu
from jax.sharding import PartitionSpec as P

H = 32
DH = 128
BLK = 128
NPOS = 16
NTK = 2.0
SIDE = 4
HEADS = 2
T = 2048
TQ = 256
CK = 512
NEG = -1e30
SCALE = 1.0 / math.sqrt(DH)
SCALE2 = SCALE * math.log2(math.e)
F32 = jnp.float32
BF16 = jnp.bfloat16
MESH_ID = pl.DeviceIdType.MESH

RING = (1, 3, 2)


def trig_tables():
    third = 2 * (DH // 6)
    dims = (DH - 2 * third, third, third)
    cos_t = np.zeros((3 * NPOS, DH), np.float32)
    sin_t = np.zeros((3 * NPOS, DH), np.float32)
    lane = 0
    for axis, dim in enumerate(dims):
        base = 10000.0 * NTK ** (dim / (dim - 2.0))
        pair = np.arange(dim // 2, dtype=np.float32)
        inverse = np.exp(pair * np.float32(-2.0 * math.log(base) / dim)).astype(np.float32)
        angle = np.arange(NPOS, dtype=np.float32)[:, None] * inverse[None, :]
        c = np.cos(angle.astype(np.float64)).astype(np.float32)
        s = np.sin(angle.astype(np.float64)).astype(np.float32)
        rows = slice(axis * NPOS, (axis + 1) * NPOS)
        cos_t[rows, lane : lane + dim] = np.repeat(c, 2, axis=1)
        sin_t[rows, lane : lane + dim : 2] = -s
        sin_t[rows, lane + 1 : lane + dim : 2] = s
        lane += dim

    def parts(table):
        out, rest = [], table
        for _ in range(3):
            piece = rest.astype(jnp.bfloat16)
            out.append(piece)
            rest = rest - piece.astype(np.float32)
        return out

    return np.stack(parts(cos_t) + parts(sin_t), 0)


def dot(a, b, ca, cb):
    return lax.dot_general(a, b, (((ca,), (cb,)), ((), ())), preferred_element_type=F32)


def swap_pairs(x):
    even = lax.broadcasted_iota(jnp.int32, x.shape, 1) % 2 == 0
    return jnp.where(even, pltpu.roll(x, DH - 1, 1), pltpu.roll(x, 1, 1))


def kernel(
    q_in, k_in, v_in, g_in, pos_ref, flag_ref, band_ref, trig_ref,
    o_out, dq_out, dk_out, dv_out,
    stage, out, relay, land, res, cos_sc, sin_sc, bias, wexp, s_sc, w_all, inv_sc, dk_acc, dv_acc,
    stage_sem, send_sem, recv_sem, own_sem,
):
    clip = lax.axis_index("clip")
    me = lax.axis_index("seq")
    x, y = me // SIDE, me % SIDE
    ins = (q_in, k_in, v_in, g_in)

    def stage_copy(a, n):
        owner, h = n // HEADS, n % HEADS
        return pltpu.make_async_copy(
            ins[a].at[:, n * DH : (n + 1) * DH],
            stage.at[a, owner // SIDE, owner % SIDE, h],
            stage_sem.at[a, n],
        )


    def bring(h, pair):
        for a in pair:
            for n in range(h, H, HEADS):
                stage_copy(a, n).start()

    def brought(h, pair):
        for a in pair:
            for n in range(h, H, HEADS):
                stage_copy(a, n).wait()

    first, second = (0, 1), (2, 3)
    barrier = pltpu.get_barrier_semaphore()
    for j in RING:
        for peer in (((x + j) % SIDE) * SIDE + y, x * SIDE + (y + j) % SIDE):
            pl.semaphore_signal(barrier, inc=1, device_id=(clip, peer), device_id_type=MESH_ID)
    bring(0, first)
    pl.semaphore_wait(barrier, 2 * len(RING))

    def ends(way, h, a, leg, along_x, idx):
        if leg == 0:
            if way == 0:
                src = stage.at[a, idx, :, h] if along_x else stage.at[a, :, idx, h]
            else:
                src = res.at[h, a, idx] if along_x else res.at[h, a, :, idx]
            return src, relay.at[way, h, a, :, x if along_x else y]
        src = relay.at[way, h, a, idx]
        if way == 0:
            return src, land.at[h, a, x] if along_x else land.at[h, a, :, y]
        return src, out.at[a, x, :, h] if along_x else out.at[a, :, y, h]

    def copies(way, h, a, leg):
        along_x = (a % 2 == 0) == (leg == 0)
        made = []
        for n, j in enumerate(RING):
            idx = (x + j) % SIDE if along_x else (y + j) % SIDE
            peer = idx * SIDE + y if along_x else x * SIDE + idx
            src, dst = ends(way, h, a, leg, along_x, idx)
            made.append(
                pltpu.make_async_remote_copy(
                    src_ref=src,
                    dst_ref=dst,
                    send_sem=send_sem.at[way, h, a, leg, n],
                    recv_sem=recv_sem.at[way, h, a, leg, n],
                    device_id=(clip, peer),
                    device_id_type=MESH_ID,
                )
            )
        return made

    def own_copy(way, h, a, leg):
        along_x = (a % 2 == 0) == (leg == 0)
        src, dst = ends(way, h, a, leg, along_x, x if along_x else y)
        return pltpu.make_async_copy(src, dst, own_sem.at[way, h, a, leg])

    def start(way, h, pair, leg):
        made = [copies(way, h, a, leg) for a in pair]
        for n in range(len(RING)):
            for remote in made:
                remote[n].start()
        for a in pair:
            own_copy(way, h, a, leg).start()

    def arrived(way, h, pair, leg):
        for a in pair:
            for c in copies(way, h, a, leg):
                c.wait_recv()
            own_copy(way, h, a, leg).wait()

    bring(0, second)
    brought(0, first)
    start(0, 0, first, 0)
    brought(0, second)
    start(0, 0, second, 0)
    bring(1, first + second)

    value = lax.broadcasted_iota(jnp.int32, (3 * NPOS, TQ), 0)

    def table_rows(t, _):
        at = pl.ds(pl.multiple_of(t * TQ, TQ), TQ)
        p = pos_ref[:, at]
        want = jnp.where(
            value < NPOS, p[0:1, :], jnp.where(value < 2 * NPOS, p[1:2, :] + NPOS, p[2:3, :] + 2 * NPOS)
        )
        hot = jnp.where(value == want, 1.0, 0.0).astype(BF16)
        cos_sc[at, :] = sum(dot(hot, trig_ref[j], 0, 0) for j in range(3))
        sin_sc[at, :] = sum(dot(hot, trig_ref[3 + j], 0, 0) for j in range(3))
        return 0

    lax.fori_loop(0, T // TQ, table_rows, 0)

    blocks = T // BLK
    band = band_ref[...]
    width = jnp.where(band == 0, 128.0, jnp.where(band == 1, 64.0, jnp.where(band == 2, 32.0, 16.0)))
    width = jnp.where(flag_ref[...] == 1, width, 0.0).astype(BF16)
    spread = lax.broadcasted_iota(jnp.int32, (blocks, T), 0) == (
        lax.broadcasted_iota(jnp.int32, (blocks, T), 1) // BLK
    )
    wexp[...] = dot(width, jnp.where(spread, 1.0, 0.0).astype(BF16), 1, 0)
    apart = jnp.abs(
        lax.broadcasted_iota(jnp.int32, (BLK, BLK), 0) - lax.broadcasted_iota(jnp.int32, (BLK, BLK), 1)
    ).astype(F32)

    def bias_rows(t, _):
        reach = wexp[pl.ds(t, 1), :]
        at = pl.ds(pl.multiple_of(t * BLK, BLK), BLK)
        for j in range(blocks):
            bias[at, j * BLK : (j + 1) * BLK] = jnp.where(
                apart < reach[:, j * BLK : (j + 1) * BLK], 0.0, NEG
            ).astype(BF16)
        return 0

    lax.fori_loop(0, blocks, bias_rows, 0)

    arrived(0, 0, first, 0)
    start(0, 0, first, 1)
    arrived(0, 0, second, 0)
    start(0, 0, second, 1)
    brought(1, first + second)
    start(0, 1, first, 0)
    start(0, 1, second, 0)

    def tile_of(ref, h, a, t):
        return ref.at[h, a, t // 2, pl.ds((t % 2) * 2, 2)]

    def load_tile(ref, h, a, t):
        return tile_of(ref, h, a, t)[...].reshape(TQ, DH)

    def chunk(h, a, c):
        return land[h, a, c].reshape(CK, DH)

    def rows_at(t):
        return pl.ds(pl.multiple_of(t * TQ, TQ), TQ)

    def run_hooks(hooks, t):
        for when, job in hooks.items():
            @pl.when(t == when)
            def _(job=job):
                job()

    def scores_pass(h, hooks):
        arrived(0, h, first, 1)

        def turn(t, _):
            at = rows_at(t)
            for a in (0, 1):
                v = load_tile(land, h, a, t).astype(F32)
                v = v * cos_sc[at, :] + swap_pairs(v) * sin_sc[at, :]
                tile_of(land, h, a, t)[...] = v.astype(BF16).reshape(2, BLK, DH)
            return 0

        lax.fori_loop(0, T // TQ, turn, 0)

        def tile(t, _):
            run_hooks(hooks, t)
            at = rows_at(t)
            q = load_tile(land, h, 0, t)
            high = jnp.full((TQ, 128), -jnp.inf, F32)
            for c in range(T // CK):
                cs = pl.ds(c * CK, CK)
                s = dot(q, chunk(h, 1, c), 1, 1) + bias[at, cs].astype(F32)
                s_sc[:, cs] = s
                for j in range(CK // 128):
                    high = jnp.maximum(high, s[:, j * 128 : (j + 1) * 128])
            m = jnp.max(high, axis=1, keepdims=True)
            total = jnp.zeros((TQ, 128), F32)
            for c in range(T // CK):
                cs = pl.ds(c * CK, CK)
                w = jnp.exp2((s_sc[:, cs] - m) * SCALE2)
                for j in range(CK // 128):
                    total = total + w[:, j * 128 : (j + 1) * 128]
                w_all[at, cs] = w.astype(BF16)
            inv = 1.0 / jnp.sum(total, axis=1, keepdims=True)
            inv_sc[at, :] = jnp.broadcast_to(inv, (TQ, 128))
            return 0

        lax.fori_loop(0, T // TQ, tile, 0)

    def grads_pass(h, hooks):
        arrived(0, h, second, 1)
        dk_acc[...] = jnp.zeros_like(dk_acc)
        dv_acc[...] = jnp.zeros_like(dv_acc)

        def tile(t, _):
            run_hooks(hooks, t)
            at = rows_at(t)
            q = load_tile(land, h, 0, t)
            g = load_tile(land, h, 3, t)
            inv = inv_sc[at, :]
            o = jnp.zeros((TQ, DH), F32)
            for c in range(T // CK):
                o = o + dot(w_all[at, pl.ds(c * CK, CK)], chunk(h, 2, c), 1, 0)
            gf = g.astype(F32)
            ob = (o * inv).astype(BF16)
            tile_of(res, h, 0, t)[...] = ob.reshape(2, BLK, DH)
            gn = gf * inv
            delta = jnp.sum(gn * ob.astype(F32), axis=1, keepdims=True)
            gn = gn.astype(BF16)
            gt, qt = gn.T, q.T
            dq = jnp.zeros((TQ, DH), F32)
            for c in range(T // CK):
                cs = pl.ds(c * CK, CK)
                dp = dot(gn, chunk(h, 2, c), 1, 1)
                wb = w_all[at, cs]
                ds = (wb.astype(F32) * (dp - delta)).astype(BF16)
                dq = dq + dot(ds, chunk(h, 1, c), 1, 0)
                dv_acc[:, cs] += dot(gt, wb, 1, 0)
                dk_acc[:, cs] += dot(qt, ds, 1, 0)
            dq = dq * SCALE
            dq = dq * cos_sc[at, :] - swap_pairs(dq) * sin_sc[at, :]
            tile_of(res, h, 1, t)[...] = dq.astype(BF16).reshape(2, BLK, DH)
            return 0

        lax.fori_loop(0, T // TQ, tile, 0)
        for t in range(T // TQ):
            cs = pl.ds(t * TQ, TQ)
            dk = dk_acc[:, cs].T * SCALE
            dk = dk * cos_sc[cs, :] - swap_pairs(dk) * sin_sc[cs, :]
            tile_of(res, h, 2, t)[...] = dk.astype(BF16).reshape(2, BLK, DH)
            tile_of(res, h, 3, t)[...] = dv_acc[:, cs].T.astype(BF16).reshape(2, BLK, DH)

    def forward(way, h, pair):
        def job():
            arrived(way, h, pair, 0)
            start(way, h, pair, 1)

        return job

    scores_pass(0, {})
    grads_pass(0, {2: forward(0, 1, first), 4: forward(0, 1, second)})
    start(1, 0, first, 0)
    start(1, 0, second, 0)
    scores_pass(1, {6: forward(1, 0, first)})
    grads_pass(1, {2: forward(1, 0, second)})
    start(1, 1, first, 0)
    start(1, 1, second, 0)
    forward(1, 1, first)()
    forward(1, 1, second)()

    outs = (o_out, dq_out, dk_out, dv_out)
    for h in range(HEADS):
        for pair in (first, second):
            arrived(1, h, pair, 1)
            for a in pair:
                for n in range(h, H, HEADS):
                    owner = n // HEADS
                    outs[a][:, n * DH : (n + 1) * DH] = out[a, owner // SIDE, owner % SIDE, h]
    for h in range(HEADS):
        for way in range(2):
            for a in range(4):
                for leg in range(2):
                    for c in copies(way, h, a, leg):
                        c.wait_send()


def write_out(o, dq, dk, dv, o_out, dq_out, dk_out, dv_out, sem):
    made = [
        pltpu.make_async_copy(src, dst, sem.at[n])
        for n, (src, dst) in enumerate(((o, o_out), (dq, dq_out), (dk, dk_out), (dv, dv_out)))
    ]
    for c in made:
        c.start()
    for c in made:
        c.wait()


def body(query_in, key_in, value_in, grad_out, positions, block_flags, band_ids):
    shape = query_in.shape
    any_spec = pl.BlockSpec(memory_space=pl.ANY)
    vmem = pl.BlockSpec(memory_space=pltpu.VMEM)
    hops = pltpu.SemaphoreType.DMA((2, HEADS, 4, 2, len(RING)))
    grid = (HEADS, 4, SIDE, SIDE, BLK, DH)
    results = pl.pallas_call(
        kernel,
        name="attention_exchange",
        out_shape=[pltpu.VMEM(shape, BF16)] * 4,
        in_specs=[any_spec] * 4 + [vmem] * 4,
        out_specs=[vmem] * 4,
        scratch_shapes=[
            pltpu.VMEM((4, SIDE, SIDE, HEADS, BLK, DH), BF16),
            pltpu.VMEM((4, SIDE, SIDE, HEADS, BLK, DH), BF16),
            pltpu.VMEM((2,) + grid, BF16),
            pltpu.VMEM(grid, BF16),
            pltpu.VMEM(grid, BF16),
            pltpu.VMEM((T, DH), F32),
            pltpu.VMEM((T, DH), F32),
            pltpu.VMEM((T, T), BF16),
            pltpu.VMEM((T // BLK, T), F32),
            pltpu.VMEM((TQ, T), F32),
            pltpu.VMEM((T, T), BF16),
            pltpu.VMEM((T, 128), F32),
            pltpu.VMEM((DH, T), F32),
            pltpu.VMEM((DH, T), F32),
            pltpu.SemaphoreType.DMA((4, H)),
            hops,
            hops,
            pltpu.SemaphoreType.DMA((2, HEADS, 4, 2)),
        ],
        compiler_params=pltpu.CompilerParams(
            collective_id=0, has_side_effects=True, vmem_limit_bytes=56000 * 1024
        ),
    )(query_in, key_in, value_in, grad_out, positions, block_flags, band_ids, jnp.asarray(trig_tables()))
    return tuple(
        pl.pallas_call(
            write_out,
            name="write_out",
            out_shape=[jax.ShapeDtypeStruct(shape, BF16)] * 4,
            in_specs=[vmem] * 4,
            out_specs=[any_spec] * 4,
            scratch_shapes=[pltpu.SemaphoreType.DMA((4,))],
            compiler_params=pltpu.CompilerParams(vmem_limit_bytes=4 * 1024 * 1024),
        )(*(pltpu.with_memory_space_constraint(r, pltpu.VMEM) for r in results))
    )


def solution(mesh):
    spec = P(("clip", "seq"), None)
    return jax.shard_map(
        body,
        mesh=mesh,
        in_specs=(spec, spec, spec, spec, P(None, "clip"), P("clip", None), P("clip", None)),
        out_specs=(spec, spec, spec, spec),
        check_vma=False,
    )
```

```python
import functools
import math

import jax
import jax.numpy as jnp
import numpy as np
from jax import lax
from jax.experimental import pallas as pl
from jax.experimental.pallas import tpu as pltpu
from jax.sharding import PartitionSpec as P

H = 32
DH = 128
BLK = 128
NPOS = 16
NTK = 2.0
SIDE = 4
HEADS = 2
T = 2048
TQ = 256
CK = 512
NEG = -1e30
SCALE = 1.0 / math.sqrt(DH)
SCALE2 = SCALE * math.log2(math.e)
F32 = jnp.float32
BF16 = jnp.bfloat16
MESH_ID = pl.DeviceIdType.MESH

RING = (1, 3, 2)


def trig_tables():
    third = 2 * (DH // 6)
    dims = (DH - 2 * third, third, third)
    cos_t = np.zeros((3 * NPOS, DH), np.float32)
    sin_t = np.zeros((3 * NPOS, DH), np.float32)
    lane = 0
    for axis, dim in enumerate(dims):
        base = 10000.0 * NTK ** (dim / (dim - 2.0))
        pair = np.arange(dim // 2, dtype=np.float32)
        inverse = np.exp(pair * np.float32(-2.0 * math.log(base) / dim)).astype(np.float32)
        angle = np.arange(NPOS, dtype=np.float32)[:, None] * inverse[None, :]
        c = np.cos(angle.astype(np.float64)).astype(np.float32)
        s = np.sin(angle.astype(np.float64)).astype(np.float32)
        rows = slice(axis * NPOS, (axis + 1) * NPOS)
        cos_t[rows, lane : lane + dim] = np.repeat(c, 2, axis=1)
        sin_t[rows, lane : lane + dim : 2] = -s
        sin_t[rows, lane + 1 : lane + dim : 2] = s
        lane += dim

    def parts(table):
        out, rest = [], table
        for _ in range(3):
            piece = rest.astype(jnp.bfloat16)
            out.append(piece)
            rest = rest - piece.astype(np.float32)
        return out

    return np.stack(parts(cos_t) + parts(sin_t), 0)


def dot(a, b, ca, cb):
    return lax.dot_general(a, b, (((ca,), (cb,)), ((), ())), preferred_element_type=F32)


def swap_pairs(x):
    even = lax.broadcasted_iota(jnp.int32, x.shape, 1) % 2 == 0
    return jnp.where(even, pltpu.roll(x, DH - 1, 1), pltpu.roll(x, 1, 1))


def kernel(
    q_in, k_in, v_in, g_in, pos_in, flag_in, band_in, trig_in,
    o_out, dq_out, dk_out, dv_out,
    stage, out, relay, land, res, cos_sc, sin_sc, bias, wexp, s_sc, w_all, inv_sc, dk_acc, dv_acc,
    pos_ref, flag_ref, band_ref, trig_ref,
    stage_sem, send_sem, recv_sem, own_sem, small_sem,
):
    clip = lax.axis_index("clip")
    me = lax.axis_index("seq")
    x, y = me // SIDE, me % SIDE
    ins = (q_in, k_in, v_in, g_in)

    def stage_copy(a, n):
        owner, h = n // HEADS, n % HEADS
        return pltpu.make_async_copy(
            ins[a].at[:, n * DH : (n + 1) * DH],
            stage.at[a, owner // SIDE, owner % SIDE, h],
            stage_sem.at[a, n],
        )


    def bring(h, pair):
        for a in pair:
            for n in range(h, H, HEADS):
                stage_copy(a, n).start()

    def brought(h, pair):
        for a in pair:
            for n in range(h, H, HEADS):
                stage_copy(a, n).wait()

    first, second = (0, 1), (2, 3)
    barrier = pltpu.get_barrier_semaphore()
    for j in RING:
        for peer in (((x + j) % SIDE) * SIDE + y, x * SIDE + (y + j) % SIDE):
            pl.semaphore_signal(barrier, inc=1, device_id=(clip, peer), device_id_type=MESH_ID)
    bring(0, first)
    small = [
        pltpu.make_async_copy(src, dst, small_sem.at[n])
        for n, (src, dst) in enumerate(
            ((pos_in, pos_ref), (flag_in, flag_ref), (band_in, band_ref), (trig_in, trig_ref))
        )
    ]
    for c in small:
        c.start()
    pl.semaphore_wait(barrier, 2 * len(RING))

    def ends(way, h, a, leg, along_x, idx):
        if leg == 0:
            if way == 0:
                src = stage.at[a, idx, :, h] if along_x else stage.at[a, :, idx, h]
            else:
                src = res.at[h, a, idx] if along_x else res.at[h, a, :, idx]
            return src, relay.at[way, h, a, :, x if along_x else y]
        src = relay.at[way, h, a, idx]
        if way == 0:
            return src, land.at[h, a, x] if along_x else land.at[h, a, :, y]
        return src, out.at[a, x, :, h] if along_x else out.at[a, :, y, h]

    def copies(way, h, a, leg):
        along_x = (a % 2 == 0) == (leg == 0)
        made = []
        for n, j in enumerate(RING):
            idx = (x + j) % SIDE if along_x else (y + j) % SIDE
            peer = idx * SIDE + y if along_x else x * SIDE + idx
            src, dst = ends(way, h, a, leg, along_x, idx)
            made.append(
                pltpu.make_async_remote_copy(
                    src_ref=src,
                    dst_ref=dst,
                    send_sem=send_sem.at[way, h, a, leg, n],
                    recv_sem=recv_sem.at[way, h, a, leg, n],
                    device_id=(clip, peer),
                    device_id_type=MESH_ID,
                )
            )
        return made

    def own_copy(way, h, a, leg):
        along_x = (a % 2 == 0) == (leg == 0)
        src, dst = ends(way, h, a, leg, along_x, x if along_x else y)
        return pltpu.make_async_copy(src, dst, own_sem.at[way, h, a, leg])

    def start(way, h, pair, leg):
        made = [copies(way, h, a, leg) for a in pair]
        for n in range(len(RING)):
            for remote in made:
                remote[n].start()
        for a in pair:
            own_copy(way, h, a, leg).start()

    def arrived(way, h, pair, leg):
        for a in pair:
            for c in copies(way, h, a, leg):
                c.wait_recv()
            own_copy(way, h, a, leg).wait()

    bring(0, second)
    brought(0, first)
    start(0, 0, first, 0)
    brought(0, second)
    start(0, 0, second, 0)
    bring(1, first + second)

    for c in small:
        c.wait()

    value = lax.broadcasted_iota(jnp.int32, (3 * NPOS, TQ), 0)

    def table_rows(t, _):
        at = pl.ds(pl.multiple_of(t * TQ, TQ), TQ)
        p = pos_ref[:, at]
        want = jnp.where(
            value < NPOS, p[0:1, :], jnp.where(value < 2 * NPOS, p[1:2, :] + NPOS, p[2:3, :] + 2 * NPOS)
        )
        hot = jnp.where(value == want, 1.0, 0.0).astype(BF16)
        cos_sc[at, :] = sum(dot(hot, trig_ref[j], 0, 0) for j in range(3))
        sin_sc[at, :] = sum(dot(hot, trig_ref[3 + j], 0, 0) for j in range(3))
        return 0

    lax.fori_loop(0, T // TQ, table_rows, 0)

    blocks = T // BLK
    band = band_ref[...]
    width = jnp.where(band == 0, 128.0, jnp.where(band == 1, 64.0, jnp.where(band == 2, 32.0, 16.0)))
    width = jnp.where(flag_ref[...] == 1, width, 0.0).astype(BF16)
    spread = lax.broadcasted_iota(jnp.int32, (blocks, T), 0) == (
        lax.broadcasted_iota(jnp.int32, (blocks, T), 1) // BLK
    )
    wexp[...] = dot(width, jnp.where(spread, 1.0, 0.0).astype(BF16), 1, 0)
    apart = jnp.abs(
        lax.broadcasted_iota(jnp.int32, (BLK, BLK), 0) - lax.broadcasted_iota(jnp.int32, (BLK, BLK), 1)
    ).astype(F32)

    def bias_rows(t, _):
        reach = wexp[pl.ds(t, 1), :]
        at = pl.ds(pl.multiple_of(t * BLK, BLK), BLK)
        for j in range(blocks):
            bias[at, j * BLK : (j + 1) * BLK] = jnp.where(
                apart < reach[:, j * BLK : (j + 1) * BLK], 0.0, NEG
            ).astype(BF16)
        return 0

    lax.fori_loop(0, blocks, bias_rows, 0)

    arrived(0, 0, first, 0)
    start(0, 0, first, 1)
    arrived(0, 0, second, 0)
    start(0, 0, second, 1)
    brought(1, first + second)
    start(0, 1, first, 0)
    start(0, 1, second, 0)

    def tile_of(ref, h, a, t):
        return ref.at[h, a, t // 2, pl.ds((t % 2) * 2, 2)]

    def load_tile(ref, h, a, t):
        return tile_of(ref, h, a, t)[...].reshape(TQ, DH)

    def chunk(h, a, c):
        return land[h, a, c].reshape(CK, DH)

    def rows_at(t):
        return pl.ds(pl.multiple_of(t * TQ, TQ), TQ)

    def run_hooks(hooks, t):
        for when, job in hooks.items():
            @pl.when(t == when)
            def _(job=job):
                job()

    def scores_pass(h, hooks):
        arrived(0, h, first, 1)

        def turn(t, _):
            at = rows_at(t)
            for a in (0, 1):
                v = load_tile(land, h, a, t).astype(F32)
                v = v * cos_sc[at, :] + swap_pairs(v) * sin_sc[at, :]
                tile_of(land, h, a, t)[...] = v.astype(BF16).reshape(2, BLK, DH)
            return 0

        lax.fori_loop(0, T // TQ, turn, 0)

        def tile(t, _):
            run_hooks(hooks, t)
            at = rows_at(t)
            q = load_tile(land, h, 0, t)
            high = jnp.full((TQ, 128), -jnp.inf, F32)
            for c in range(T // CK):
                cs = pl.ds(c * CK, CK)
                s = dot(q, chunk(h, 1, c), 1, 1) + bias[at, cs].astype(F32)
                s_sc[:, cs] = s
                for j in range(CK // 128):
                    high = jnp.maximum(high, s[:, j * 128 : (j + 1) * 128])
            m = jnp.max(high, axis=1, keepdims=True)
            total = jnp.zeros((TQ, 128), F32)
            for c in range(T // CK):
                cs = pl.ds(c * CK, CK)
                w = jnp.exp2((s_sc[:, cs] - m) * SCALE2)
                for j in range(CK // 128):
                    total = total + w[:, j * 128 : (j + 1) * 128]
                w_all[at, cs] = w.astype(BF16)
            inv = 1.0 / jnp.sum(total, axis=1, keepdims=True)
            inv_sc[at, :] = jnp.broadcast_to(inv, (TQ, 128))
            return 0

        lax.fori_loop(0, T // TQ, tile, 0)

    def grads_pass(h, hooks):
        arrived(0, h, second, 1)
        dk_acc[...] = jnp.zeros_like(dk_acc)
        dv_acc[...] = jnp.zeros_like(dv_acc)

        def tile(t, _):
            run_hooks(hooks, t)
            at = rows_at(t)
            q = load_tile(land, h, 0, t)
            g = load_tile(land, h, 3, t)
            inv = inv_sc[at, :]
            o = jnp.zeros((TQ, DH), F32)
            for c in range(T // CK):
                o = o + dot(w_all[at, pl.ds(c * CK, CK)], chunk(h, 2, c), 1, 0)
            gf = g.astype(F32)
            ob = (o * inv).astype(BF16)
            tile_of(res, h, 0, t)[...] = ob.reshape(2, BLK, DH)
            gn = gf * inv
            delta = jnp.sum(gn * ob.astype(F32), axis=1, keepdims=True)
            gn = gn.astype(BF16)
            gt, qt = gn.T, q.T
            dq = jnp.zeros((TQ, DH), F32)
            for c in range(T // CK):
                cs = pl.ds(c * CK, CK)
                dp = dot(gn, chunk(h, 2, c), 1, 1)
                wb = w_all[at, cs]
                ds = (wb.astype(F32) * (dp - delta)).astype(BF16)
                dq = dq + dot(ds, chunk(h, 1, c), 1, 0)
                dv_acc[:, cs] += dot(gt, wb, 1, 0)
                dk_acc[:, cs] += dot(qt, ds, 1, 0)
            dq = dq * SCALE
            dq = dq * cos_sc[at, :] - swap_pairs(dq) * sin_sc[at, :]
            tile_of(res, h, 1, t)[...] = dq.astype(BF16).reshape(2, BLK, DH)
            return 0

        lax.fori_loop(0, T // TQ, tile, 0)
        for t in range(T // TQ):
            cs = pl.ds(t * TQ, TQ)
            dk = dk_acc[:, cs].T * SCALE
            dk = dk * cos_sc[cs, :] - swap_pairs(dk) * sin_sc[cs, :]
            tile_of(res, h, 2, t)[...] = dk.astype(BF16).reshape(2, BLK, DH)
            tile_of(res, h, 3, t)[...] = dv_acc[:, cs].T.astype(BF16).reshape(2, BLK, DH)

    def forward(way, h, pair):
        def job():
            arrived(way, h, pair, 0)
            start(way, h, pair, 1)

        return job

    scores_pass(0, {})
    grads_pass(0, {3: forward(0, 1, first), 5: forward(0, 1, second)})
    start(1, 0, first, 0)
    start(1, 0, second, 0)
    scores_pass(1, {7: forward(1, 0, first)})
    grads_pass(1, {3: forward(1, 0, second)})
    start(1, 1, first, 0)
    start(1, 1, second, 0)
    forward(1, 1, first)()
    forward(1, 1, second)()

    outs = (o_out, dq_out, dk_out, dv_out)
    for h in range(HEADS):
        for pair in (first, second):
            arrived(1, h, pair, 1)
            for a in pair:
                for n in range(h, H, HEADS):
                    owner = n // HEADS
                    outs[a][:, n * DH : (n + 1) * DH] = out[a, owner // SIDE, owner % SIDE, h]
    for h in range(HEADS):
        for way in range(2):
            for a in range(4):
                for leg in range(2):
                    for c in copies(way, h, a, leg):
                        c.wait_send()


def write_out(o, dq, dk, dv, o_out, dq_out, dk_out, dv_out, sem):
    made = [
        pltpu.make_async_copy(src, dst, sem.at[n])
        for n, (src, dst) in enumerate(((o, o_out), (dq, dq_out), (dk, dk_out), (dv, dv_out)))
    ]
    for c in made:
        c.start()
    for c in made:
        c.wait()


def body(query_in, key_in, value_in, grad_out, positions, block_flags, band_ids):
    shape = query_in.shape
    any_spec = pl.BlockSpec(memory_space=pl.ANY)
    vmem = pl.BlockSpec(memory_space=pltpu.VMEM)
    trig = jnp.asarray(trig_tables())
    hops = pltpu.SemaphoreType.DMA((2, HEADS, 4, 2, len(RING)))
    grid = (HEADS, 4, SIDE, SIDE, BLK, DH)
    results = pl.pallas_call(
        kernel,
        name="attention_exchange",
        out_shape=[pltpu.VMEM(shape, BF16)] * 4,
        in_specs=[any_spec] * 8,
        out_specs=[vmem] * 4,
        scratch_shapes=[
            pltpu.VMEM((4, SIDE, SIDE, HEADS, BLK, DH), BF16),
            pltpu.VMEM((4, SIDE, SIDE, HEADS, BLK, DH), BF16),
            pltpu.VMEM((2,) + grid, BF16),
            pltpu.VMEM(grid, BF16),
            pltpu.VMEM(grid, BF16),
            pltpu.VMEM((T, DH), F32),
            pltpu.VMEM((T, DH), F32),
            pltpu.VMEM((T, T), BF16),
            pltpu.VMEM((T // BLK, T), F32),
            pltpu.VMEM((TQ, T), F32),
            pltpu.VMEM((T, T), BF16),
            pltpu.VMEM((T, 128), F32),
            pltpu.VMEM((DH, T), F32),
            pltpu.VMEM((DH, T), F32),
            pltpu.VMEM(positions.shape, jnp.int32),
            pltpu.VMEM(block_flags.shape, jnp.int32),
            pltpu.VMEM(band_ids.shape, jnp.int32),
            pltpu.VMEM(trig.shape, BF16),
            pltpu.SemaphoreType.DMA((4, H)),
            hops,
            hops,
            pltpu.SemaphoreType.DMA((2, HEADS, 4, 2)),
            pltpu.SemaphoreType.DMA((4,)),
        ],
        compiler_params=pltpu.CompilerParams(
            collective_id=0, has_side_effects=True, vmem_limit_bytes=56000 * 1024
        ),
    )(query_in, key_in, value_in, grad_out, positions, block_flags, band_ids, trig)
    return tuple(
        pl.pallas_call(
            write_out,
            name="write_out",
            out_shape=[jax.ShapeDtypeStruct(shape, BF16)] * 4,
            in_specs=[vmem] * 4,
            out_specs=[any_spec] * 4,
            scratch_shapes=[pltpu.SemaphoreType.DMA((4,))],
            compiler_params=pltpu.CompilerParams(vmem_limit_bytes=4 * 1024 * 1024),
        )(*(pltpu.with_memory_space_constraint(r, pltpu.VMEM) for r in results))
    )


def solution(mesh):
    spec = P(("clip", "seq"), None)
    return jax.shard_map(
        body,
        mesh=mesh,
        in_specs=(spec, spec, spec, spec, P(None, "clip"), P("clip", None), P("clip", None)),
        out_specs=(spec, spec, spec, spec),
        check_vma=False,
    )
```

```python
import functools
import math

import jax
import jax.numpy as jnp
import numpy as np
from jax import lax
from jax.experimental import pallas as pl
from jax.experimental.pallas import tpu as pltpu
from jax.sharding import PartitionSpec as P

H = 32
DH = 128
BLK = 128
NPOS = 16
NTK = 2.0
SIDE = 4
HEADS = 2
T = 2048
TQ = 256
CK = 512
NEG = -1e30
SCALE = 1.0 / math.sqrt(DH)
SCALE2 = SCALE * math.log2(math.e)
F32 = jnp.float32
BF16 = jnp.bfloat16
MESH_ID = pl.DeviceIdType.MESH

RING = (1, 3, 2)


def trig_tables():
    third = 2 * (DH // 6)
    dims = (DH - 2 * third, third, third)
    cos_t = np.zeros((3 * NPOS, DH), np.float32)
    sin_t = np.zeros((3 * NPOS, DH), np.float32)
    lane = 0
    for axis, dim in enumerate(dims):
        base = 10000.0 * NTK ** (dim / (dim - 2.0))
        pair = np.arange(dim // 2, dtype=np.float32)
        inverse = np.exp(pair * np.float32(-2.0 * math.log(base) / dim)).astype(np.float32)
        angle = np.arange(NPOS, dtype=np.float32)[:, None] * inverse[None, :]
        c = np.cos(angle.astype(np.float64)).astype(np.float32)
        s = np.sin(angle.astype(np.float64)).astype(np.float32)
        rows = slice(axis * NPOS, (axis + 1) * NPOS)
        cos_t[rows, lane : lane + dim] = np.repeat(c, 2, axis=1)
        sin_t[rows, lane : lane + dim : 2] = -s
        sin_t[rows, lane + 1 : lane + dim : 2] = s
        lane += dim

    def parts(table):
        out, rest = [], table
        for _ in range(3):
            piece = rest.astype(jnp.bfloat16)
            out.append(piece)
            rest = rest - piece.astype(np.float32)
        return out

    return np.stack(parts(cos_t) + parts(sin_t), 0)


def dot(a, b, ca, cb):
    return lax.dot_general(a, b, (((ca,), (cb,)), ((), ())), preferred_element_type=F32)


def swap_pairs(x):
    even = lax.broadcasted_iota(jnp.int32, x.shape, 1) % 2 == 0
    return jnp.where(even, pltpu.roll(x, DH - 1, 1), pltpu.roll(x, 1, 1))


def kernel(
    q_in, k_in, v_in, g_in, pos_in, flag_in, band_in, trig_in,
    o_out, dq_out, dk_out, dv_out,
    stage, out, relay, land, res, cos_sc, sin_sc, bias, wexp, s_sc, w_all, inv_sc, dk_acc, dv_acc,
    pos_ref, flag_ref, band_ref, trig_ref,
    stage_sem, send_sem, recv_sem, own_sem, small_sem,
):
    clip = lax.axis_index("clip")
    me = lax.axis_index("seq")
    x, y = me // SIDE, me % SIDE
    ins = (q_in, k_in, v_in, g_in)

    def stage_copy(a, n):
        owner, h = n // HEADS, n % HEADS
        return pltpu.make_async_copy(
            ins[a].at[:, n * DH : (n + 1) * DH],
            stage.at[a, owner // SIDE, owner % SIDE, h],
            stage_sem.at[a, n],
        )


    def bring(h, pair):
        for a in pair:
            for n in range(h, H, HEADS):
                stage_copy(a, n).start()

    def brought(h, pair):
        for a in pair:
            for n in range(h, H, HEADS):
                stage_copy(a, n).wait()

    first, second = (0, 1), (2, 3)
    barrier = pltpu.get_barrier_semaphore()
    for j in RING:
        for peer in (((x + j) % SIDE) * SIDE + y, x * SIDE + (y + j) % SIDE):
            pl.semaphore_signal(barrier, inc=1, device_id=(clip, peer), device_id_type=MESH_ID)
    bring(0, first)
    small = [
        pltpu.make_async_copy(src, dst, small_sem.at[n])
        for n, (src, dst) in enumerate(
            ((pos_in, pos_ref), (flag_in, flag_ref), (band_in, band_ref), (trig_in, trig_ref))
        )
    ]
    for c in small:
        c.start()
    pl.semaphore_wait(barrier, 2 * len(RING))

    def ends(way, h, a, leg, along_x, idx):
        if leg == 0:
            if way == 0:
                src = stage.at[a, idx, :, h] if along_x else stage.at[a, :, idx, h]
            else:
                src = res.at[h, a, idx] if along_x else res.at[h, a, :, idx]
            return src, relay.at[way, h, a, :, x if along_x else y]
        src = relay.at[way, h, a, idx]
        if way == 0:
            return src, land.at[h, a, x] if along_x else land.at[h, a, :, y]
        return src, out.at[a, x, :, h] if along_x else out.at[a, :, y, h]

    def copies(way, h, a, leg):
        along_x = (a % 2 == 0) == (leg == 0)
        made = []
        for n, j in enumerate(RING):
            idx = (x + j) % SIDE if along_x else (y + j) % SIDE
            peer = idx * SIDE + y if along_x else x * SIDE + idx
            src, dst = ends(way, h, a, leg, along_x, idx)
            made.append(
                pltpu.make_async_remote_copy(
                    src_ref=src,
                    dst_ref=dst,
                    send_sem=send_sem.at[way, h, a, leg, n],
                    recv_sem=recv_sem.at[way, h, a, leg, n],
                    device_id=(clip, peer),
                    device_id_type=MESH_ID,
                )
            )
        return made

    def own_copy(way, h, a, leg):
        along_x = (a % 2 == 0) == (leg == 0)
        src, dst = ends(way, h, a, leg, along_x, x if along_x else y)
        return pltpu.make_async_copy(src, dst, own_sem.at[way, h, a, leg])

    def start(way, h, pair, leg):
        made = [copies(way, h, a, leg) for a in pair]
        for n in range(len(RING)):
            for remote in made:
                remote[n].start()
        for a in pair:
            own_copy(way, h, a, leg).start()

    def arrived(way, h, pair, leg):
        for a in pair:
            for c in copies(way, h, a, leg):
                c.wait_recv()
            own_copy(way, h, a, leg).wait()

    bring(0, second)
    brought(0, first)
    start(0, 0, first, 0)
    brought(0, second)
    start(0, 0, second, 0)
    bring(1, first + second)

    for c in small:
        c.wait()

    value = lax.broadcasted_iota(jnp.int32, (3 * NPOS, TQ), 0)

    def table_rows(t, _):
        at = pl.ds(pl.multiple_of(t * TQ, TQ), TQ)
        p = pos_ref[:, at]
        want = jnp.where(
            value < NPOS, p[0:1, :], jnp.where(value < 2 * NPOS, p[1:2, :] + NPOS, p[2:3, :] + 2 * NPOS)
        )
        hot = jnp.where(value == want, 1.0, 0.0).astype(BF16)
        cos_sc[at, :] = sum(dot(hot, trig_ref[j], 0, 0) for j in range(3))
        sin_sc[at, :] = sum(dot(hot, trig_ref[3 + j], 0, 0) for j in range(3))
        return 0

    lax.fori_loop(0, T // TQ, table_rows, 0)

    blocks = T // BLK
    band = band_ref[...]
    width = jnp.where(band == 0, 128.0, jnp.where(band == 1, 64.0, jnp.where(band == 2, 32.0, 16.0)))
    width = jnp.where(flag_ref[...] == 1, width, 0.0).astype(BF16)
    spread = lax.broadcasted_iota(jnp.int32, (blocks, T), 0) == (
        lax.broadcasted_iota(jnp.int32, (blocks, T), 1) // BLK
    )
    wexp[...] = dot(width, jnp.where(spread, 1.0, 0.0).astype(BF16), 1, 0)
    apart = jnp.abs(
        lax.broadcasted_iota(jnp.int32, (BLK, BLK), 0) - lax.broadcasted_iota(jnp.int32, (BLK, BLK), 1)
    ).astype(F32)

    def bias_rows(t, _):
        reach = wexp[pl.ds(t, 1), :]
        at = pl.ds(pl.multiple_of(t * BLK, BLK), BLK)
        for j in range(blocks):
            bias[at, j * BLK : (j + 1) * BLK] = jnp.where(
                apart < reach[:, j * BLK : (j + 1) * BLK], 0.0, NEG
            ).astype(BF16)
        return 0

    lax.fori_loop(0, blocks, bias_rows, 0)

    arrived(0, 0, first, 0)
    start(0, 0, first, 1)
    arrived(0, 0, second, 0)
    start(0, 0, second, 1)
    brought(1, first + second)
    start(0, 1, first, 0)
    start(0, 1, second, 0)

    def tile_of(ref, h, a, t):
        return ref.at[h, a, t // 2, pl.ds((t % 2) * 2, 2)]

    def load_tile(ref, h, a, t):
        return tile_of(ref, h, a, t)[...].reshape(TQ, DH)

    def chunk(h, a, c):
        return land[h, a, c].reshape(CK, DH)

    def rows_at(t):
        return pl.ds(pl.multiple_of(t * TQ, TQ), TQ)

    def run_hooks(hooks, t):
        for when, job in hooks.items():
            @pl.when(t == when)
            def _(job=job):
                job()

    def scores_pass(h, hooks):
        arrived(0, h, first, 1)

        def turn(t, _):
            at = rows_at(t)
            for a in (0, 1):
                v = load_tile(land, h, a, t).astype(F32)
                v = v * cos_sc[at, :] + swap_pairs(v) * sin_sc[at, :]
                tile_of(land, h, a, t)[...] = v.astype(BF16).reshape(2, BLK, DH)
            return 0

        lax.fori_loop(0, T // TQ, turn, 0)

        def tile(t, _):
            run_hooks(hooks, t)
            at = rows_at(t)
            q = load_tile(land, h, 0, t)
            high = jnp.full((TQ, 128), -jnp.inf, F32)
            for c in range(T // CK):
                cs = pl.ds(c * CK, CK)
                s = dot(q, chunk(h, 1, c), 1, 1) + bias[at, cs].astype(F32)
                s_sc[:, cs] = s
                for j in range(CK // 128):
                    high = jnp.maximum(high, s[:, j * 128 : (j + 1) * 128])
            m = jnp.max(high, axis=1, keepdims=True)
            total = jnp.zeros((TQ, 128), F32)
            for c in range(T // CK):
                cs = pl.ds(c * CK, CK)
                w = jnp.exp2((s_sc[:, cs] - m) * SCALE2)
                for j in range(CK // 128):
                    total = total + w[:, j * 128 : (j + 1) * 128]
                w_all[at, cs] = w.astype(BF16)
            inv = 1.0 / jnp.sum(total, axis=1, keepdims=True)
            inv_sc[at, :] = jnp.broadcast_to(inv, (TQ, 128))
            return 0

        lax.fori_loop(0, T // TQ, tile, 0)

    def grads_pass(h, hooks):
        arrived(0, h, second, 1)
        dk_acc[...] = jnp.zeros_like(dk_acc)
        dv_acc[...] = jnp.zeros_like(dv_acc)

        def tile(t, _):
            run_hooks(hooks, t)
            at = rows_at(t)
            q = load_tile(land, h, 0, t)
            g = load_tile(land, h, 3, t)
            inv = inv_sc[at, :]
            o = jnp.zeros((TQ, DH), F32)
            for c in range(T // CK):
                o = o + dot(w_all[at, pl.ds(c * CK, CK)], chunk(h, 2, c), 1, 0)
            gf = g.astype(F32)
            ob = (o * inv).astype(BF16)
            tile_of(res, h, 0, t)[...] = ob.reshape(2, BLK, DH)
            gn = gf * inv
            delta = jnp.sum(gn * ob.astype(F32), axis=1, keepdims=True)
            gn = gn.astype(BF16)
            gt, qt = gn.T, q.T
            dq = jnp.zeros((TQ, DH), F32)
            for c in range(T // CK):
                cs = pl.ds(c * CK, CK)
                dp = dot(gn, chunk(h, 2, c), 1, 1)
                wb = w_all[at, cs]
                ds = (wb.astype(F32) * (dp - delta)).astype(BF16)
                dq = dq + dot(ds, chunk(h, 1, c), 1, 0)
                dv_acc[:, cs] += dot(gt, wb, 1, 0)
                dk_acc[:, cs] += dot(qt, ds, 1, 0)
            dq = dq * SCALE
            dq = dq * cos_sc[at, :] - swap_pairs(dq) * sin_sc[at, :]
            tile_of(res, h, 1, t)[...] = dq.astype(BF16).reshape(2, BLK, DH)
            return 0

        lax.fori_loop(0, T // TQ, tile, 0)
        for t in range(T // TQ):
            cs = pl.ds(t * TQ, TQ)
            dk = dk_acc[:, cs].T * SCALE
            dk = dk * cos_sc[cs, :] - swap_pairs(dk) * sin_sc[cs, :]
            tile_of(res, h, 2, t)[...] = dk.astype(BF16).reshape(2, BLK, DH)
            tile_of(res, h, 3, t)[...] = dv_acc[:, cs].T.astype(BF16).reshape(2, BLK, DH)
            if t == 1:
                start(1, h, first, 0)

    def forward(way, h, pair):
        def job():
            arrived(way, h, pair, 0)
            start(way, h, pair, 1)

        return job

    scores_pass(0, {})
    grads_pass(0, {3: forward(0, 1, first), 5: forward(0, 1, second)})
    start(1, 0, second, 0)
    scores_pass(1, {7: forward(1, 0, first)})
    grads_pass(1, {3: forward(1, 0, second)})
    start(1, 1, second, 0)
    forward(1, 1, first)()
    forward(1, 1, second)()

    outs = (o_out, dq_out, dk_out, dv_out)
    for h in range(HEADS):
        for pair in (first, second):
            arrived(1, h, pair, 1)
            for a in pair:
                for n in range(h, H, HEADS):
                    owner = n // HEADS
                    outs[a][:, n * DH : (n + 1) * DH] = out[a, owner // SIDE, owner % SIDE, h]
    for h in range(HEADS):
        for way in range(2):
            for a in range(4):
                for leg in range(2):
                    for c in copies(way, h, a, leg):
                        c.wait_send()


def write_out(o, dq, dk, dv, o_out, dq_out, dk_out, dv_out, sem):
    made = [
        pltpu.make_async_copy(src, dst, sem.at[n])
        for n, (src, dst) in enumerate(((o, o_out), (dq, dq_out), (dk, dk_out), (dv, dv_out)))
    ]
    for c in made:
        c.start()
    for c in made:
        c.wait()


def body(query_in, key_in, value_in, grad_out, positions, block_flags, band_ids):
    shape = query_in.shape
    any_spec = pl.BlockSpec(memory_space=pl.ANY)
    vmem = pl.BlockSpec(memory_space=pltpu.VMEM)
    trig = jnp.asarray(trig_tables())
    hops = pltpu.SemaphoreType.DMA((2, HEADS, 4, 2, len(RING)))
    grid = (HEADS, 4, SIDE, SIDE, BLK, DH)
    results = pl.pallas_call(
        kernel,
        name="attention_exchange",
        out_shape=[pltpu.VMEM(shape, BF16)] * 4,
        in_specs=[any_spec] * 8,
        out_specs=[vmem] * 4,
        scratch_shapes=[
            pltpu.VMEM((4, SIDE, SIDE, HEADS, BLK, DH), BF16),
            pltpu.VMEM((4, SIDE, SIDE, HEADS, BLK, DH), BF16),
            pltpu.VMEM((2,) + grid, BF16),
            pltpu.VMEM(grid, BF16),
            pltpu.VMEM(grid, BF16),
            pltpu.VMEM((T, DH), F32),
            pltpu.VMEM((T, DH), F32),
            pltpu.VMEM((T, T), BF16),
            pltpu.VMEM((T // BLK, T), F32),
            pltpu.VMEM((TQ, T), F32),
            pltpu.VMEM((T, T), BF16),
            pltpu.VMEM((T, 128), F32),
            pltpu.VMEM((DH, T), F32),
            pltpu.VMEM((DH, T), F32),
            pltpu.VMEM(positions.shape, jnp.int32),
            pltpu.VMEM(block_flags.shape, jnp.int32),
            pltpu.VMEM(band_ids.shape, jnp.int32),
            pltpu.VMEM(trig.shape, BF16),
            pltpu.SemaphoreType.DMA((4, H)),
            hops,
            hops,
            pltpu.SemaphoreType.DMA((2, HEADS, 4, 2)),
            pltpu.SemaphoreType.DMA((4,)),
        ],
        compiler_params=pltpu.CompilerParams(
            collective_id=0, has_side_effects=True, vmem_limit_bytes=56000 * 1024
        ),
    )(query_in, key_in, value_in, grad_out, positions, block_flags, band_ids, trig)
    return tuple(
        pl.pallas_call(
            write_out,
            name="write_out",
            out_shape=[jax.ShapeDtypeStruct(shape, BF16)] * 4,
            in_specs=[vmem] * 4,
            out_specs=[any_spec] * 4,
            scratch_shapes=[pltpu.SemaphoreType.DMA((4,))],
            compiler_params=pltpu.CompilerParams(vmem_limit_bytes=4 * 1024 * 1024),
        )(*(pltpu.with_memory_space_constraint(r, pltpu.VMEM) for r in results))
    )


def solution(mesh):
    spec = P(("clip", "seq"), None)
    return jax.shard_map(
        body,
        mesh=mesh,
        in_specs=(spec, spec, spec, spec, P(None, "clip"), P("clip", None), P("clip", None)),
        out_specs=(spec, spec, spec, spec),
        check_vma=False,
    )
```
